256 devices in a mesh: grp: 2 (over z_lo), dp: 32 (over y, z_hi, core), mp: 4 (over x).
Axes of the slice: x: 4, y: 4, z: 8 (z_hi: 4, z_lo: 2; z = z_hi * 2 + z_lo), core: 2. Of those that a mesh axis runs over, the one named last changes fastest.
Arguments:
- up_input: bfloat16 [64, 256, 4096], P(('grp', 'dp'), None, 'mp'), may hold values from -6 to 6
- gate_pre: bfloat16 [64, 256, 14336], P(('grp', 'dp'), None, 'mp'), may hold values from -6 to 6
- up_pre: bfloat16 [64, 256, 14336], P(('grp', 'dp'), None, 'mp'), may hold values from -6 to 6
- grad_hidden: bfloat16 [64, 256, 14336], P(('grp', 'dp'), None, 'mp'), may hold values from -6 to 6
- grad_output: bfloat16 [64, 256, 4096], P(('grp', 'dp'), None, 'mp'), may hold values from -6 to 6
- proj_up_in: bfloat16 [64, 4096], P(None, 'mp'), may hold values from -0.09375 to 0.09375
- proj_up_out: bfloat16 [64, 14336], P(None, 'mp'), may hold values from -0.046875 to 0.046875
- proj_down_in: bfloat16 [64, 14336], P(None, 'mp'), may hold values from -0.046875 to 0.046875
- proj_down_out: bfloat16 [64, 4096], P(None, 'mp'), may hold values from -0.09375 to 0.09375
- gram: float32 [8192, 8192], P(('grp', 'mp'), 'dp'), may hold values from -4 to 14
- canaries: bfloat16 [1024, 8192], P('dp', ('grp', 'mp')), may hold values from -6 to 6
Outputs:
- gram_new: float32 [8192, 8192], P(('grp', 'mp'), 'dp')
- mapped: bfloat16 [1024, 8192], P(('grp', 'mp'), 'dp')
- scores: float32 [64, 1024], P(None, ('grp', 'mp'))
The draws below stay inside these ranges and needn't reach their ends.
All inputs are finite; a program needn't handle non-finite values.
Results may differ from the reference program's by a relative error of at most 0.005.
Values may be sent and summed in bfloat16 or wider, within the bound.
A program may use at most 64 MiB of HBM per device.

```python
import math
import jax
import jax.numpy as jnp
from jax import lax

D = 4096
FF = 14336
RANK = 64
SEQ = 256
CAN = 1024
SEQS = 64
ORDER = 8192


def draw_gram(key, part):
    first, second = jax.random.split(jax.random.fold_in(key, 17), 2)
    base = jnp.clip(jax.random.normal(first, (ORDER, ORDER), jnp.float32), -4.0, 4.0)
    symmetric = 0.5 * (base + base.T)
    diagonal = jnp.exp(jax.random.uniform(second, (ORDER,), jnp.float32, 0.0, math.log(10.0)))
    return symmetric + jnp.diag(diagonal)


def block_levels(stream_key, extent, shards, smallest, top_value):
    def one(axis_at, shards_of):
        steps = jax.random.uniform(jax.random.fold_in(jax.random.fold_in(stream_key, 6), axis_at), (shards_of,), jnp.float32, smallest / len(shards), top_value / len(shards))
        return jnp.repeat(jnp.exp(steps), extent[axis_at] // shards_of).reshape((-1,) + (1,) * (len(extent) - axis_at - 1))

    factor_of = one(*shards[0])
    for cut in shards[1:]:
        factor_of = factor_of * one(*cut)
    return factor_of


def scatter_about(own_key, dims, spread, limit, cuts=(), dtype=jnp.bfloat16):
    entries = spread * jax.random.normal(own_key, dims, jnp.float32)
    if cuts:
        entries = entries * block_levels(own_key, dims, cuts, -0.22, 0.18)
    return jnp.clip(entries, -limit, limit).astype(dtype)


def setup_inputs(seed: int = 0) -> dict:
    key_of = jax.random.split(jax.random.key(seed), 12)
    up_input = scatter_about(key_of[0], (SEQS, SEQ, D), 1.0, 6.0, ((0, 64), (2, 4)))
    gate_pre = scatter_about(key_of[1], (SEQS, SEQ, FF), 1.0, 6.0, ((0, 64), (2, 4)))
    up_pre = scatter_about(key_of[2], (SEQS, SEQ, FF), 1.0, 6.0, ((0, 64), (2, 4)))
    grad_hidden = scatter_about(key_of[3], (SEQS, SEQ, FF), 1.0, 6.0, ((0, 64), (2, 4)))
    grad_output = scatter_about(key_of[4], (SEQS, SEQ, D), 1.0, 6.0, ((0, 64), (2, 4)))
    proj_up_in = scatter_about(key_of[5], (RANK, D), D ** -0.5, 0.09375, ((1, 4),))
    proj_up_out = scatter_about(key_of[6], (RANK, FF), FF ** -0.5, 0.046875, ((1, 4),))
    proj_down_in = scatter_about(key_of[7], (RANK, FF), FF ** -0.5, 0.046875, ((1, 4),))
    proj_down_out = scatter_about(key_of[8], (RANK, D), D ** -0.5, 0.09375, ((1, 4),))
    gram = draw_gram(jax.random.fold_in(key_of[11], 71), 0)
    canaries = scatter_about(key_of[10], (CAN, ORDER), 1.0, 6.0, ((0, 32), (1, 8)))
    return {"up_input": up_input, "gate_pre": gate_pre, "up_pre": up_pre, "grad_hidden": grad_hidden, "grad_output": grad_output, "proj_up_in": proj_up_in, "proj_up_out": proj_up_out, "proj_down_in": proj_down_in, "proj_down_out": proj_down_out, "gram": gram, "canaries": canaries}


def project(values, matrix):
    return lax.dot_general(values, matrix, (((1,), (1,)), ((), ())), preferred_element_type=jnp.float32)

def sequence_row(pieces, proj_up_in, proj_up_out, proj_down_in, proj_down_out):
    up_input, gate_pre, up_pre, grad_hidden, grad_output = pieces
    gate_act = jax.nn.silu(gate_pre.astype(jnp.float32))
    grad_up = (grad_hidden.astype(jnp.float32) * gate_act).astype(jnp.bfloat16)
    hidden = (gate_act * up_pre.astype(jnp.float32)).astype(jnp.bfloat16)
    in_up = project(up_input, proj_up_in)
    out_up = project(grad_up, proj_up_out)
    in_down = project(hidden, proj_down_in)
    out_down = project(grad_output, proj_down_out)
    norm_len = 1.0 / math.sqrt(SEQ)
    up_feat = jnp.dot(out_up.T, in_up, precision=lax.Precision.HIGHEST) * norm_len
    down_feat = jnp.dot(out_down.T, in_down, precision=lax.Precision.HIGHEST) * norm_len
    return jnp.concatenate([up_feat.reshape(-1), down_feat.reshape(-1)])

def reference(up_input, gate_pre, up_pre, grad_hidden, grad_output, proj_up_in, proj_up_out, proj_down_in, proj_down_out, gram, canaries):

    def one_row(pieces):
        return sequence_row(pieces, proj_up_in, proj_up_out, proj_down_in, proj_down_out)
    features = lax.map(one_row, (up_input, gate_pre, up_pre, grad_hidden, grad_output))
    gram_new = gram + jnp.dot(features.T, features, precision=lax.Precision.HIGHEST) / SEQS
    gram_low = gram_new.astype(jnp.bfloat16)
    norm_order = 1.0 / math.sqrt(ORDER)
    mapped_full = jnp.dot(canaries, gram_low, preferred_element_type=jnp.float32) * norm_order
    scores = jnp.dot(features, mapped_full.T, precision=lax.Precision.HIGHEST) * norm_order
    return (gram_new, mapped_full.astype(jnp.bfloat16), scores)
```

```python
import functools
import math

import jax
import jax.numpy as jnp
from jax import lax
from jax.experimental import pallas as pl
from jax.experimental.pallas import tpu as pltpu
from jax.sharding import Mesh
from jax.sharding import PartitionSpec as P

GRP_DP = ("g", "y", "h", "c")
DP = ("y", "h", "c")
GX = ("g", "x")
NCH = 7
ROWS = 32
HI = lax.Precision.HIGHEST
F32 = jnp.float32
BF = jnp.bfloat16
NT = (((1,), (1,)), ((), ()))
TN = (((0,), (0,)), ((), ()))

C_Z, C_Y, C_P = 0, 4, 20
A_, FZ, FY, FK, FD, PX, PZ, TX, TZ, EZ, EY, EC = 36, 42, 49, 52, 53, 60, 66, 67, 70, 71, 74, 77
SLOTS = 78


def dot_nt(a, b, precision=None):
    return lax.dot_general(a, b, NT, precision=precision, preferred_element_type=F32)


def body(
    ui, gp, up, gh, go, pui, puo, pdi, pdo, gram, can,
    gram_out, mapped_out, scores_out,
    ui_v, gp_v, up_v, gh_v, go_v, pui_v, puo_v, pdi_v, pdo_v, gram_v,
    gu_b, hid_b, acc_ou, acc_id, gram_b,
    cf, a_in, a_out, ra_in, ra_out, fz, fall, fd,
    pst, pown, rp, qst, qown, rq, ts, town, rt, tq, rtq,
    es, res, ey, rey, ec, rec, r_v, t_v, k_v,
    ls, ss, rs, fdr,
):
    g, y, h, c, x = (lax.axis_index(n) for n in ("g", "y", "h", "c", "x"))
    z = h * 2 + g
    oc = 1 - c
    og = 1 - g

    def rem(v, n):
        return lax.rem(v, n)

    bar = pltpu.get_barrier_semaphore()

    def greet(**dev):
        pl.semaphore_signal(bar, inc=1, device_id=dev, device_id_type=pl.DeviceIdType.MESH)

    for r in range(1, 4):
        greet(x=rem(x + r, 4))
        greet(x=rem(x + r, 4), c=oc)
        greet(y=rem(y + r, 4))
    for r in range(1, 8):
        zz = rem(z + r, 8)
        greet(h=zz // 2, g=rem(zz, 2))
    greet(c=oc)

    loads = []

    def load(src, dst):
        cp = pltpu.make_async_copy(src, dst, ls.at[len(loads)])
        cp.start()
        loads.append(cp)
        return cp

    blk = lambda yy, hh, cc: (yy * 4 + hh) * 2 + cc
    l_c = load(can, cf.at[blk(y, h, c)])
    l_ch = []
    l_puo = load(puo, puo_v)
    l_pdi = load(pdi, pdi_v)
    for k in range(NCH):
        s = pl.ds(k * 512, 512)
        l_ch.append([load(a.at[0, :, s], b.at[k]) for a, b in ((gp, gp_v), (gh, gh_v), (up, up_v))])
    l_in = [load(a, b) for a, b in ((pui, pui_v), (ui.at[0], ui_v), (pdo, pdo_v), (go.at[0], go_v))]
    l_g = load(gram, gram_v)

    sent = []

    def rcopy(src, dst, slot, **dev):
        return pltpu.make_async_remote_copy(
            src_ref=src, dst_ref=dst, send_sem=ss.at[slot], recv_sem=rs.at[slot],
            device_id=dev, device_id_type=pl.DeviceIdType.MESH,
        )

    live = {}

    def send(src, dst, slot, **dev):
        cp = rcopy(src, dst, slot, **dev)
        cp.start()
        live[slot] = cp

    def got(slot):
        live[slot].wait_recv()

    def chunk(k):
        for cp in l_ch[k]:
            cp.wait()
        if k == 0:
            l_puo.wait()
            l_pdi.wait()

        def tile(i, _):
            rows = pl.ds(i * ROWS, ROWS)
            v = gp_v[k, rows, :].astype(F32)
            act = v / (1.0 + jnp.exp(-v))
            gu_b[rows, :] = (gh_v[k, rows, :].astype(F32) * act).astype(BF)
            hid_b[rows, :] = (act * up_v[k, rows, :].astype(F32)).astype(BF)
            return 0

        lax.fori_loop(0, 256 // ROWS, tile, 0)
        s = slice(k * 512, (k + 1) * 512)
        ou = dot_nt(puo_v[:, s], gu_b[...])
        idn = dot_nt(pdi_v[:, s], hid_b[...])
        if k == 0:
            acc_ou[...] = ou
            acc_id[...] = idn
        else:
            acc_ou[...] += ou
            acc_id[...] += idn

    hp, hm, h2 = rem(h + 1, 4), rem(h + 3, 4), rem(h + 2, 4)
    yp, ym, y2 = rem(y + 1, 4), rem(y + 3, 4), rem(y + 2, 4)
    hk = (h, hm, hp, h2)
    yj = (y, ym, yp, y2)
    lo, hi = pl.ds(0, 16), pl.ds(16, 16)

    def whole(b):
        return cf.at[b]

    def partner(j, k):
        b = blk(yj[j], hk[k], c)
        send(whole(b), whole(b), C_P + j * 4 + k, c=oc)

    def spread(k):
        b = blk(y, hk[k], c)
        send(whole(b), whole(b), C_Y + k, y=yp)
        send(whole(b), whole(b), C_Y + 4 + k, y=ym)
        partner(0, k)

    def c_start():
        b = blk(y, h, c)
        l_c.wait()
        send(whole(b), whole(b), C_Z, h=hp)
        send(whole(b), whole(b), C_Z + 1, h=hm)
        spread(0)

    def c_z1():
        got(C_Z)
        b = blk(y, hm, c)
        send(cf.at[b, lo], cf.at[b, lo], C_Z + 2, h=hp)
        spread(1)
        got(C_Z + 1)
        b = blk(y, hp, c)
        send(cf.at[b, hi], cf.at[b, hi], C_Z + 3, h=hm)
        spread(2)

    def c_z2():
        got(C_Z + 2)
        got(C_Z + 3)
        spread(3)

    def c_y1(k):
        got(C_Y + k)
        b = blk(ym, hk[k], c)
        send(cf.at[b, lo], cf.at[b, lo], C_Y + 8 + k, y=yp)
        partner(1, k)
        got(C_Y + 4 + k)
        b = blk(yp, hk[k], c)
        send(cf.at[b, hi], cf.at[b, hi], C_Y + 12 + k, y=ym)
        partner(2, k)

    def c_y2(k):
        got(C_Y + 8 + k)
        got(C_Y + 12 + k)
        partner(3, k)

    chunk(0)
    chunk(1)
    pl.semaphore_wait(bar, 17)
    c_start()
    for k in range(2, 5):
        chunk(k)
    c_z1()
    for k in range(5, NCH):
        chunk(k)
    for cp in l_in:
        cp.wait()
    iu = dot_nt(pui_v[...], ui_v[...])
    od = dot_nt(pdo_v[...], go_v[...])
    idn = acc_id[...]
    ou = acc_ou[...]

    a_in[0] = iu.astype(BF)
    a_in[1] = idn.astype(BF)
    a_out[:, 0] = ou.reshape(4, 16, 256)
    a_out[:, 1] = od.reshape(4, 16, 256)
    for r in range(1, 4):
        xp = rem(x + r, 4)
        send(a_in, ra_in.at[r - 1], A_ + 2 * (r - 1), x=xp)
        send(a_out.at[xp], ra_out.at[r - 1], A_ + 2 * (r - 1) + 1, x=xp)
    c_z2()
    l_g.wait()
    gram_b[...] = gram_v[...].astype(BF)

    lane = lax.broadcasted_iota(jnp.int32, (64, 1024), 1)
    tile_m = jnp.where(lane % 64 == lax.broadcasted_iota(jnp.int32, (64, 1024), 0), 1.0, 0.0).astype(BF)
    lane16 = lax.broadcasted_iota(jnp.int32, (16, 1024), 1)
    mask16 = lane16 // 64 == lax.broadcasted_iota(jnp.int32, (16, 1024), 0)

    for r in range(3):
        got(A_ + 2 * r)
        got(A_ + 2 * r + 1)
    for m, own in ((0, iu), (1, idn)):
        ins, outs = own, a_out[x, m]
        for r in range(3):
            ins = ins + ra_in[r, m].astype(F32)
            outs = outs + ra_out[r, m]
        feat = dot_nt(outs, ins, HI) * (1.0 / 16.0)
        spreadf = jnp.dot(feat.astype(BF), tile_m, preferred_element_type=F32)
        row = jnp.sum(jnp.where(mask16, spreadf, 0.0), axis=0, keepdims=True)
        fz[pl.ds(z, 1), m * 1024 : (m + 1) * 1024] = row

    for r in range(1, 8):
        zz = rem(z + r, 8)
        send(fz.at[pl.ds(z, 1)], fz.at[pl.ds(z, 1)], FZ + r - 1, h=zz // 2, g=rem(zz, 2))
    for k in range(4):
        c_y1(k)
    for r in range(7):
        got(FZ + r)
    fall[y, c] = fz[...].astype(BF)
    for r in range(1, 4):
        send(fall.at[y, c], fall.at[y, c], FY + r - 1, y=rem(y + r, 4))
    for k in range(4):
        c_y2(k)
    for j in range(4):
        for k in range(4):
            got(C_P + j * 4 + k)

    def rows_of(b):
        return cf[pl.ds(4 * b, 4)].reshape(128, 1024)

    def times_gram(b):
        return jnp.dot(rows_of(b), gram_b[...], preferred_element_type=F32)

    for r in range(1, 4):
        xp = rem(x + r, 4)
        for q in range(2):
            pst[r - 1, q] = times_gram(q * 4 + xp).astype(BF)
            send(pst.at[r - 1, q], rp.at[r - 1, q], PX + 2 * (r - 1) + q, x=xp)
    for r in range(3):
        got(FY + r)
    gl = pl.ds(pl.multiple_of(g * 1024, 1024), 1024)
    send(fall.at[:, c, :, gl], fall.at[:, c, :, gl], FK, c=oc)
    x_src = 2 * rem(y, 2) + h // 2
    base = (y // 2) * 1024 + rem(h, 2) * 512

    def fd_copies():
        def piece(cc):
            return fall.at[:, c, :, pl.ds(pl.multiple_of(base + cc * 256, 256), 256)]

        def to(i, cc, **dev):
            return pltpu.make_async_remote_copy(
                src_ref=piece(cc), dst_ref=fd.at[:, c], send_sem=ss.at[FD + i], recv_sem=fdr.at[c],
                device_id=dev, device_id_type=pl.DeviceIdType.MESH,
            )

        cps = []
        for r in range(1, 4):
            xp = rem(x + r, 4)
            cps.append(to(2 * r - 2, c, x=xp))
            cps.append(to(2 * r - 1, oc, x=xp, c=oc))
        cps.append(to(6, oc, c=oc))
        own = pltpu.make_async_copy(piece(c), fd.at[:, c], ls.at[len(loads)])
        return cps, own

    @pl.when(x == x_src)
    def _():
        cps, own = fd_copies()
        for cp in cps:
            cp.start()
        own.start()

    for q in range(2):
        pown[q] = times_gram(q * 4 + x)

    got(FK)
    fk32 = fall[:, :, :, gl].astype(F32).reshape(64, 1024)
    fk = fk32.astype(BF)
    ft = dot_nt(fk, cf[...].reshape(1024, 1024))
    fkk = dot_nt(fk, jnp.concatenate([fk, fk], axis=0))
    for b in range(8):
        town[b % 4, b // 4] = ft[:, b * 128 : (b + 1) * 128]
        ts[b % 4, b // 4] = ft[:, b * 128 : (b + 1) * 128].astype(BF)
    k_v[...] = fkk
    for b in range(4):
        ts[b, 2] = fkk.astype(BF)
    for r in range(1, 4):
        xp = rem(x + r, 4)
        send(ts.at[xp], rt.at[r - 1], TX + r - 1, x=xp)

    for r in range(6):
        got(PX + r)
    for q in range(2):
        acc = pown[q]
        for r in range(3):
            acc = acc + rp[r, q].astype(F32)
        qown[q] = acc
    qst[...] = qown[og].astype(BF)
    send(qst, rq, PZ, g=og)

    @pl.when(x == x_src)
    def _():
        cps, own = fd_copies()
        own.wait()

    @pl.when(x != x_src)
    def _():
        pltpu.make_async_remote_copy(
            src_ref=fd.at[:, c], dst_ref=fd.at[:, c], send_sem=ss.at[FD], recv_sem=fdr.at[c],
            device_id={"c": oc}, device_id_type=pl.DeviceIdType.MESH,
        ).wait_recv()

    pltpu.make_async_remote_copy(
        src_ref=fd.at[:, oc], dst_ref=fd.at[:, oc], send_sem=ss.at[FD], recv_sem=fdr.at[oc],
        device_id={"c": oc}, device_id_type=pl.DeviceIdType.MESH,
    ).wait_recv()
    fd32 = fd[...].astype(F32).reshape(64, 256)
    fdb = fd32.astype(BF)

    got(PZ)
    rr = qown[g] + rq[...].astype(F32)
    r_v[...] = rr
    r_hi = rr.astype(BF)
    r_lo = (rr - r_hi.astype(F32)).astype(BF)
    s1 = dot_nt(fdb, r_hi) + dot_nt(fdb, r_lo)
    ey[...] = s1
    es[...] = s1.astype(BF)
    for r in range(1, 4):
        send(es, res.at[r - 1], EZ + r - 1, h=rem(h + r, 4))

    for r in range(3):
        got(TX + r)
    for q in range(2):
        acc = town[x, q]
        for r in range(3):
            acc = acc + rt[r, q].astype(F32)
        town[x, q] = acc
    acc = k_v[...]
    for r in range(3):
        acc = acc + rt[r, 2].astype(F32)
    k_v[...] = acc
    tq[0] = town[x, og].astype(BF)
    tq[1] = acc.astype(BF)
    send(tq, rtq, TZ, g=og)

    for i in range(4):
        rows = slice(i * 256, (i + 1) * 256)
        gram_out[rows, :] = gram_v[rows, :] + lax.dot_general(
            fk[:, rows], fdb, TN, preferred_element_type=F32
        ) * (1.0 / 64.0)

    for r in range(3):
        got(EZ + r)
    acc = ey[...]
    for r in range(3):
        acc = acc + res[r].astype(F32)
    ec[...] = acc
    for r in range(1, 4):
        send(ec, rey.at[r - 1], EY + r - 1, y=rem(y + r, 4))

    got(TZ)
    t_f = town[x, g] + rtq[0].astype(F32)
    k_f = (k_v[...] + rtq[1].astype(F32))[:, :64]
    norm = 1.0 / math.sqrt(8192.0)
    tf = lax.dot_general(t_f, fd32, TN, precision=HI, preferred_element_type=F32)
    mapped_out[...] = ((r_v[...] + tf * (1.0 / 64.0)) * norm).astype(BF)
    kt = jnp.dot(k_f, t_f, precision=HI, preferred_element_type=F32)

    for r in range(3):
        got(EY + r)
    acc = ec[...]
    for r in range(3):
        acc = acc + rey[r]
    t_v[...] = acc
    send(t_v, rec, EC, c=oc)
    got(EC)
    total = (acc + rec[...] + kt * (1.0 / 64.0)) * (1.0 / 8192.0)
    for s in range(64):
        yy, cc, zz = s // 16, (s // 8) % 2, s % 8
        t = (zz % 2) * 32 + yy * 8 + (zz // 2) * 2 + cc
        scores_out[t : t + 1, :] = total[s : s + 1, :]

    for cp in live.values():
        cp.wait_send()

    @pl.when(x == x_src)
    def _():
        cps, own = fd_copies()
        for cp in cps:
            cp.wait_send()


def shards(*args):
    any_ = pl.BlockSpec(memory_space=pl.ANY)
    vm = pl.BlockSpec(memory_space=pltpu.VMEM)
    V = pltpu.VMEM
    scratch = [
        V((256, 1024), BF), V((NCH, 256, 512), BF), V((NCH, 256, 512), BF), V((NCH, 256, 512), BF),
        V((256, 1024), BF), V((64, 1024), BF), V((64, 3584), BF), V((64, 3584), BF), V((64, 1024), BF),
        V((1024, 256), F32),
        V((256, 512), BF), V((256, 512), BF), V((64, 256), F32), V((64, 256), F32), V((1024, 256), BF),
        V((32, 32, 1024), BF),
        V((2, 64, 256), BF), V((4, 2, 16, 256), F32), V((3, 2, 64, 256), BF), V((3, 2, 16, 256), F32),
        V((8, 2048), F32), V((4, 2, 8, 2048), BF), V((4, 2, 8, 256), BF),
        V((3, 2, 128, 256), BF), V((2, 128, 256), F32), V((3, 2, 128, 256), BF),
        V((128, 256), BF), V((2, 128, 256), F32), V((128, 256), BF),
        V((4, 3, 64, 128), BF), V((4, 2, 64, 128), F32), V((3, 3, 64, 128), BF),
        V((2, 64, 128), BF), V((2, 64, 128), BF),
        V((64, 128), BF), V((3, 64, 128), BF), V((64, 128), F32), V((3, 64, 128), F32),
        V((64, 128), F32), V((64, 128), F32), V((128, 256), F32), V((64, 128), F32), V((64, 128), F32),
        pltpu.SemaphoreType.DMA((40,)), pltpu.SemaphoreType.DMA((SLOTS,)), pltpu.SemaphoreType.DMA((SLOTS,)),
        pltpu.SemaphoreType.DMA((2,)),
    ]
    return pl.pallas_call(
        body,
        name="step",
        out_shape=(
            jax.ShapeDtypeStruct((1024, 256), F32),
            jax.ShapeDtypeStruct((128, 256), BF),
            jax.ShapeDtypeStruct((64, 128), F32),
        ),
        in_specs=[any_] * 11,
        out_specs=(vm, vm, vm),
        scratch_shapes=scratch,
        compiler_params=pltpu.CompilerParams(collective_id=0, has_side_effects=True),
    )(*args)


def solution(mesh):
    finer = Mesh(mesh.devices.reshape(2, 4, 4, 2, 4), ("g", "y", "h", "c", "x"))
    in_specs = (P(GRP_DP, None, "x"),) * 5 + (P(None, "x"),) * 4 + (P(GX, DP), P(DP, GX))
    out_specs = (P(GX, DP), P(GX, DP), P(None, GX))
    return jax.shard_map(shards, mesh=finer, in_specs=in_specs, out_specs=out_specs, check_vma=False)
```

```python
import math

import jax
import jax.numpy as jnp
from jax import lax
from jax.experimental import pallas as pl
from jax.experimental.pallas import tpu as pltpu
from jax.sharding import Mesh
from jax.sharding import PartitionSpec as P

GRP_DP = ("g", "y", "h", "c")
DP = ("y", "h", "c")
GX = ("g", "x")
NCH = 7
ROWS = 32
HI = lax.Precision.HIGHEST
F32 = jnp.float32
BF = jnp.bfloat16
NT = (((1,), (1,)), ((), ()))
TN = (((0,), (0,)), ((), ()))
MESH = pl.DeviceIdType.MESH

C_Z, C_Y, C_R, C_P = 0, 6, 22, 30
A_, FZ, FY, FK, TX, TZ, EZ, EY = 46, 58, 65, 68, 69, 72, 73, 76
SLOTS = 83


def dot_nt(a, b, precision=None):
    return lax.dot_general(a, b, NT, precision=precision, preferred_element_type=F32)


def body(
    ui, gp, up, gh, go, pui, puo, pdi, pdo, gram, can,
    fk_out, fd_out, mapped_out, scores_out,
    ui_v, gp_v, up_v, gh_v, go_v, pui_v, puo_v, pdi_v, pdo_v, gram_v,
    gu_b, hid_b, acc_ou, acc_id, gram_b,
    cf, a_in, a_out, ra_in, ra_out, fz, fown, fka, fd,
    pst, pown, rp, ts, town, rt, tq, rtq,
    es, res, ey, rey, r_v, k_v,
    ls, ss, rs, fds, fdr, ps, pr,
):
    g, y, h, c, x = (lax.axis_index(n) for n in ("g", "y", "h", "c", "x"))
    z = h * 2 + g
    oc = 1 - c
    og = 1 - g
    rem = lax.rem
    hp, hm, h2 = rem(h + 1, 4), rem(h + 3, 4), rem(h + 2, 4)
    yp, ym, y2 = rem(y + 1, 4), rem(y + 3, 4), rem(y + 2, 4)
    hk = (h, hm, hp, h2)
    yj = (y, ym, yp, y2)

    bar = pltpu.get_barrier_semaphore()
    near = [dict(y=yp), dict(y=ym), dict(h=hp), dict(h=hm), dict(g=og), dict(c=oc)]
    for r in range(1, 4):
        near += [dict(x=rem(x + r, 4)), dict(x=rem(x + r, 4), c=oc)]
    for dev in near:
        pl.semaphore_signal(bar, inc=1, device_id=dev, device_id_type=MESH)

    loads = []

    def load(src, dst):
        cp = pltpu.make_async_copy(src, dst, ls.at[len(loads)])
        cp.start()
        loads.append(cp)
        return cp

    def blk(yy, hh, cc):
        return (yy * 4 + hh) * 2 + cc

    own = blk(y, h, c)
    l_c = load(can, cf.at[own])
    l_in = [load(a, b) for a, b in ((pui, pui_v), (ui.at[0], ui_v), (pdo, pdo_v), (go.at[0], go_v))]
    l_p = [load(puo, puo_v), load(pdi, pdi_v)]
    l_ch = []
    for k in range(NCH):
        s = pl.ds(k * 512, 512)
        l_ch.append([load(a.at[0, :, s], b.at[k]) for a, b in ((gp, gp_v), (gh, gh_v), (up, up_v))])
    l_g = load(gram, gram_v)

    live = {}

    def send(src, dst, slot, **dev):
        cp = pltpu.make_async_remote_copy(
            src_ref=src, dst_ref=dst, send_sem=ss.at[slot], recv_sem=rs.at[slot],
            device_id=dev, device_id_type=MESH,
        )
        cp.start()
        live[slot] = cp

    def got(slot):
        live[slot].wait_recv()

    def chunk(k):
        for cp in l_ch[k]:
            cp.wait()

        def tile(i, _):
            rows = pl.ds(i * ROWS, ROWS)
            v = gp_v[k, rows, :].astype(F32)
            act = v / (1.0 + jnp.exp(-v))
            gu_b[rows, :] = (gh_v[k, rows, :].astype(F32) * act).astype(BF)
            hid_b[rows, :] = (act * up_v[k, rows, :].astype(F32)).astype(BF)
            return 0

        lax.fori_loop(0, 256 // ROWS, tile, 0)
        s = slice(k * 512, (k + 1) * 512)
        ou = dot_nt(puo_v[:, s], gu_b[...])
        idn = dot_nt(pdi_v[:, s], hid_b[...])
        if k == 0:
            acc_ou[...] = ou
            acc_id[...] = idn
        else:
            acc_ou[...] += ou
            acc_id[...] += idn

    half = (pl.ds(0, 16), pl.ds(16, 16))
    dirs = (yp, ym)

    def move(b, part, slot, **dev):
        ref = cf.at[b] if part is None else cf.at[b, half[part]]
        send(ref, ref, slot, **dev)

    def partner(j, k):
        move(blk(yj[j], hk[k], c), None, C_P + j * 4 + k, c=oc)

    def y_slot(d, k, part):
        return C_Y + (d * 4 + k) * 2 + part

    def spread(k, part, order=(0, 1)):
        b = blk(y, hk[k], c)
        for d in order:
            move(b, part, y_slot(d, k, part), y=dirs[d])

    def c_start():
        l_c.wait()
        move(own, 0, C_Z, h=hp)
        move(own, 1, C_Z + 2, h=hm)
        move(own, 0, y_slot(0, 0, 0), y=yp)
        move(own, 1, y_slot(1, 0, 1), y=ym)
        move(own, 1, C_Z + 1, h=hp)
        move(own, 0, C_Z + 3, h=hm)
        move(own, 1, y_slot(0, 0, 1), y=yp)
        move(own, 0, y_slot(1, 0, 0), y=ym)
        partner(0, 0)

    def c_z1():
        got(C_Z)
        move(blk(y, hm, c), 0, C_Z + 4, h=hp)
        spread(1, 0)
        got(C_Z + 2)
        move(blk(y, hp, c), 1, C_Z + 5, h=hm)
        spread(2, 1)

    def c_z2():
        got(C_Z + 1)
        spread(1, 1)
        partner(0, 1)
        got(C_Z + 3)
        spread(2, 0)
        partner(0, 2)

    def c_z3():
        got(C_Z + 4)
        spread(3, 0)
        got(C_Z + 5)
        spread(3, 1)
        partner(0, 3)

    def c_rel(k):
        got(y_slot(0, k, 0))
        move(blk(ym, hk[k], c), 0, C_R + k, y=yp)
        got(y_slot(1, k, 1))
        move(blk(yp, hk[k], c), 1, C_R + 4 + k, y=ym)

    def c_ydone(k):
        got(y_slot(0, k, 1))
        partner(1, k)
        got(y_slot(1, k, 0))
        partner(2, k)

    def c_y2(k):
        got(C_R + k)
        got(C_R + 4 + k)
        partner(3, k)

    def p_to(j, i):
        gq, xq = yj[j] // 2, 2 * rem(yj[j], 2) + i
        rel = rem(gq + g, 2) * 4 + rem(xq + 4 - x, 4)
        slot = jnp.maximum(rel - 1, 0)
        n = j * 2 + i
        cp = pltpu.make_async_remote_copy(
            src_ref=pst.at[n], dst_ref=rp.at[slot], send_sem=ps.at[n], recv_sem=pr.at[slot],
            device_id=dict(g=gq, x=xq), device_id_type=MESH,
        )
        return cp, rel

    def p_group(j):
        for k in range(4):
            got(C_P + j * 4 + k)
        for i in range(2):
            b = 2 * yj[j] + i
            prod = jnp.dot(cf[pl.ds(4 * b, 4)].reshape(128, 1024), gram_b[...], preferred_element_type=F32)
            pst[j * 2 + i] = prod.astype(BF)
            cp, rel = p_to(j, i)

            @pl.when(rel != 0)
            def _():
                cp.start()

            @pl.when(rel == 0)
            def _():
                pown[...] = prod

    for cp in l_in:
        cp.wait()
    iu = dot_nt(pui_v[...], ui_v[...])
    od = dot_nt(pdo_v[...], go_v[...])
    a_in[0] = iu.astype(BF)
    a_out[1] = od.reshape(4, 16, 256)
    for cp in l_p:
        cp.wait()
    chunk(0)
    pl.semaphore_wait(bar, len(near))
    c_start()

    def a_send(q, m_in, m_out):
        for r in range(1, 4):
            xp = rem(x + r, 4)
            send(a_in.at[m_in], ra_in.at[r - 1, m_in], A_ + q * 6 + 2 * (r - 1), x=xp)
            send(a_out.at[m_out, xp], ra_out.at[r - 1, m_out], A_ + q * 6 + 2 * (r - 1) + 1, x=xp)

    a_send(0, 0, 1)
    chunk(1)
    chunk(2)
    chunk(3)
    c_z1()
    c_rel(0)
    chunk(4)
    c_z2()
    chunk(5)
    chunk(6)
    idn = acc_id[...]
    ou = acc_ou[...]
    a_in[1] = idn.astype(BF)
    a_out[0] = ou.reshape(4, 16, 256)
    a_send(1, 1, 0)
    c_z3()
    c_ydone(0)
    c_rel(1)
    c_rel(2)
    l_g.wait()
    gram_b[...] = gram_v[...].astype(BF)
    for s in range(6):
        got(A_ + s)
    p_group(0)

    lane = lax.broadcasted_iota(jnp.int32, (64, 1024), 1)
    tile_m = jnp.where(lane % 64 == lax.broadcasted_iota(jnp.int32, (64, 1024), 0), 1.0, 0.0).astype(BF)
    lane16 = lax.broadcasted_iota(jnp.int32, (16, 1024), 1)
    mask16 = lane16 // 64 == lax.broadcasted_iota(jnp.int32, (16, 1024), 0)

    for s in range(6, 12):
        got(A_ + s)
    for m, mine in ((0, iu), (1, idn)):
        ins, outs = mine, a_out[m, x]
        for r in range(3):
            ins = ins + ra_in[r, m].astype(F32)
            outs = outs + ra_out[r, m]
        feat = dot_nt(outs, ins, HI) * (1.0 / 16.0)
        wide = jnp.dot(feat.astype(BF), tile_m, preferred_element_type=F32)
        row = jnp.sum(jnp.where(mask16, wide, 0.0), axis=0, keepdims=True)
        fz[pl.ds(z, 1), m * 1024 : (m + 1) * 1024] = row

    for r in range(1, 8):
        zz = rem(z + r, 8)
        send(fz.at[pl.ds(z, 1)], fz.at[pl.ds(z, 1)], FZ + r - 1, h=zz // 2, g=rem(zz, 2))
    c_ydone(1)
    c_ydone(2)
    c_rel(3)
    c_y2(0)
    c_y2(1)
    c_ydone(3)
    p_group(1)
    p_group(2)
    for r in range(7):
        got(FZ + r)
    fown[...] = fz[...].astype(BF)
    gl = pl.ds(pl.multiple_of(g * 1024, 1024), 1024)
    fka[y, c] = fown[:, gl]

    is_src = h // 2 == rem(x, 2)

    def fd_copies():
        remote, local = [], []
        for n in range(2):
            yt = x // 2 + 2 * n
            for r in range(4):
                for q, cc in enumerate((c, oc)):
                    i = n * 8 + r * 2 + q
                    lo = pl.multiple_of(n * 1024 + rem(h, 2) * 512 + cc * 256, 256)
                    piece = fown.at[:, pl.ds(lo, 256)]
                    cp = pltpu.make_async_remote_copy(
                        src_ref=piece, dst_ref=fd.at[y, c], send_sem=fds.at[i], recv_sem=fdr.at[y, c],
                        device_id=dict(y=yt, x=rem(x + r, 4), c=cc), device_id_type=MESH,
                    )
                    if r == 0 and q == 0:
                        remote.append((cp, yt != y))
                        local.append((pltpu.make_async_copy(piece, fd.at[y, c], fdr.at[y, c]), yt == y))
                    else:
                        remote.append((cp, None))
        return remote, local

    @pl.when(is_src)
    def _():
        remote, local = fd_copies()
        for cp, cond in remote:
            if cond is None:
                cp.start()
            else:
                pl.when(cond)(cp.start)
        for cp, cond in local:
            pl.when(cond)(cp.start)

    for r in range(1, 4):
        send(fka.at[y, c], fka.at[y, c], FY + r - 1, y=rem(y + r, 4))
    c_y2(2)
    c_y2(3)
    p_group(3)
    for r in range(3):
        got(FY + r)
    send(fka.at[:, c], fka.at[:, c], FK, c=oc)
    for yy in range(4):
        for cc in range(2):
            pltpu.make_async_copy(fd.at[yy, cc], fd.at[yy, cc], fdr.at[yy, cc]).wait()
    fd32 = fd[...].astype(F32).reshape(64, 256)
    fdb = fd32.astype(BF)
    fd_out[...] = fdb

    rr = pown[...]
    for s in range(7):
        pltpu.make_async_copy(rp.at[s], rp.at[s], pr.at[s]).wait()
        rr = rr + rp[s].astype(F32)
    r_v[...] = rr
    r_hi = rr.astype(BF)
    r_lo = (rr - r_hi.astype(F32)).astype(BF)
    s1 = dot_nt(fdb, r_hi) + dot_nt(fdb, r_lo)
    ey[...] = s1
    es[0] = s1.astype(BF)
    for r in range(1, 4):
        send(es.at[0], res.at[r - 1], EZ + r - 1, h=rem(h + r, 4))

    got(FK)
    fk = fka[...].astype(F32).reshape(64, 1024).astype(BF)
    fk_out[...] = fk
    ft = dot_nt(fk, cf[...].reshape(1024, 1024))
    fkk = dot_nt(fk, jnp.concatenate([fk, fk], axis=0))
    for b in range(8):
        town[b % 4, b // 4] = ft[:, b * 128 : (b + 1) * 128]
        ts[b % 4, b // 4] = ft[:, b * 128 : (b + 1) * 128].astype(BF)
    k_v[...] = fkk
    for b in range(4):
        ts[b, 2] = fkk.astype(BF)
    for r in range(1, 4):
        xp = rem(x + r, 4)
        send(ts.at[xp], rt.at[r - 1], TX + r - 1, x=xp)
    for r in range(3):
        got(TX + r)
    for q in range(2):
        acc = town[x, q]
        for r in range(3):
            acc = acc + rt[r, q].astype(F32)
        town[x, q] = acc
    acc = k_v[...]
    for r in range(3):
        acc = acc + rt[r, 2].astype(F32)
    k_v[...] = acc
    tq[0] = town[x, og].astype(BF)
    tq[1] = acc.astype(BF)
    send(tq, rtq, TZ, g=og)

    for r in range(3):
        got(EZ + r)
    acc = ey[...]
    for r in range(3):
        acc = acc + res[r].astype(F32)
    ey[...] = acc
    es[1] = acc.astype(BF)
    for r in range(1, 4):
        yt = rem(y + r, 4)
        send(es.at[1], rey.at[r - 1], EY + r - 1, y=yt)
        send(es.at[1], rey.at[r + 2], EY + r + 2, y=yt, c=oc)
    send(es.at[1], rey.at[6], EY + 6, c=oc)

    got(TZ)
    t_f = town[x, g] + rtq[0].astype(F32)
    k_f = (k_v[...] + rtq[1].astype(F32))[:, :64]
    norm = 1.0 / math.sqrt(8192.0)
    tf = lax.dot_general(t_f, fd32, TN, precision=HI, preferred_element_type=F32)
    mapped_out[...] = ((r_v[...] + tf * (1.0 / 64.0)) * norm).astype(BF)
    kt = jnp.dot(k_f, t_f, precision=HI, preferred_element_type=F32)

    acc = ey[...] + kt * (1.0 / 64.0)
    for s in range(7):
        got(EY + s)
        acc = acc + rey[s].astype(F32)
    scores_out[...] = acc * (1.0 / 8192.0)

    for cp in live.values():
        cp.wait_send()
    for j in range(4):
        for i in range(2):
            cp, rel = p_to(j, i)
            pl.when(rel != 0)(cp.wait_send)

    @pl.when(is_src)
    def _():
        for cp, cond in fd_copies()[0]:
            if cond is None:
                cp.wait_send()
            else:
                pl.when(cond)(cp.wait_send)


def finish(gram, fk, fd, mapped, scores, gram_out, mapped_out, scores_out, gin, gnew, sin, sout):
    def part(i):
        return pl.ds(i * 256, 256)

    ins = [pltpu.make_async_copy(gram.at[part(i)], gin.at[part(i)], sin.at[i]) for i in range(4)]
    outs = [pltpu.make_async_copy(gnew.at[part(i)], gram_out.at[part(i)], sout.at[i]) for i in range(4)]
    for cp in ins:
        cp.start()
    mapped_out[...] = mapped[...]
    for s in range(64):
        yy, cc, zz = s // 16, (s // 8) % 2, s % 8
        t = (zz % 2) * 32 + yy * 8 + (zz // 2) * 2 + cc
        scores_out[t : t + 1, :] = scores[s : s + 1, :]
    for i in range(4):
        add = lax.dot_general(fk[:, i * 256 : (i + 1) * 256], fd[...], TN, preferred_element_type=F32)
        ins[i].wait()
        gnew[part(i), :] = gin[part(i), :] + add * (1.0 / 64.0)
        outs[i].start()
    for cp in outs:
        cp.wait()


def shards(*args):
    any_ = pl.BlockSpec(memory_space=pl.ANY)
    vm = pl.BlockSpec(memory_space=pltpu.VMEM)
    V = pltpu.VMEM
    dma = pltpu.SemaphoreType.DMA
    S = jax.ShapeDtypeStruct
    scratch = [
        V((256, 1024), BF), V((NCH, 256, 512), BF), V((NCH, 256, 512), BF), V((NCH, 256, 512), BF),
        V((256, 1024), BF), V((64, 1024), BF), V((64, 3584), BF), V((64, 3584), BF), V((64, 1024), BF),
        V((1024, 256), F32),
        V((256, 512), BF), V((256, 512), BF), V((64, 256), F32), V((64, 256), F32), V((1024, 256), BF),
        V((32, 32, 1024), BF),
        V((2, 64, 256), BF), V((2, 4, 16, 256), F32), V((3, 2, 64, 256), BF), V((3, 2, 16, 256), F32),
        V((8, 2048), F32), V((8, 2048), BF), V((4, 2, 8, 1024), BF), V((4, 2, 8, 256), BF),
        V((8, 128, 256), BF), V((128, 256), F32), V((7, 128, 256), BF),
        V((4, 3, 64, 128), BF), V((4, 2, 64, 128), F32), V((3, 3, 64, 128), BF),
        V((2, 64, 128), BF), V((2, 64, 128), BF),
        V((2, 64, 128), BF), V((3, 64, 128), BF), V((64, 128), F32), V((7, 64, 128), BF),
        V((128, 256), F32), V((64, 128), F32),
        dma((40,)), dma((SLOTS,)), dma((SLOTS,)), dma((16,)), dma((4, 2)), dma((8,)), dma((7,)),
    ]
    gram = args[9]
    fk, fd, mapped, scores = pl.pallas_call(
        body,
        name="step",
        out_shape=(S((64, 1024), BF), S((64, 256), BF), S((128, 256), BF), S((64, 128), F32)),
        in_specs=[any_] * 11,
        out_specs=(vm,) * 4,
        scratch_shapes=scratch,
        compiler_params=pltpu.CompilerParams(collective_id=0, has_side_effects=True),
    )(*args)
    return pl.pallas_call(
        finish,
        name="finish",
        out_shape=(S((1024, 256), F32), S((128, 256), BF), S((64, 128), F32)),
        in_specs=[any_] + [vm] * 4,
        out_specs=(any_, vm, vm),
        scratch_shapes=[V((1024, 256), F32), V((1024, 256), F32), dma((4,)), dma((4,))],
    )(gram, fk, fd, mapped, scores)


def solution(mesh):
    finer = Mesh(mesh.devices.reshape(2, 4, 4, 2, 4), ("g", "y", "h", "c", "x"))
    in_specs = (P(GRP_DP, None, "x"),) * 5 + (P(None, "x"),) * 4 + (P(GX, DP), P(DP, GX))
    out_specs = (P(GX, DP), P(GX, DP), P(None, GX))
    return jax.shard_map(shards, mesh=finer, in_specs=in_specs, out_specs=out_specs, check_vma=False)
```
